256 devices in a mesh: branch: 64 (over z, y, x_lo), rows: 4 (over x_hi, core).
Axes of the slice: x: 4 (x_hi: 2, x_lo: 2; x = x_hi * 2 + x_lo), y: 4, z: 8, core: 2. Of those that a mesh axis runs over, the one named last changes fastest.
Arguments:
- points: float32 [3, 524288], P(None, ('branch', 'rows')), may hold values from 0 to 1, as said below
- noise: float32 [524288], P(('branch', 'rows')), may hold values from 0.2 to 2
- landmarks: float32 [7, 3, 256], replicated, may hold values from 0 to 1, as said below
- mixing: float32 [7, 256, 256], replicated, may hold values from -6 to 6
Outputs:
- bases: float32 [3, 524288, 256], P(None, ('branch', 'rows'))
- factors: float32 [64, 3, 256, 256], P('branch')
The draws below stay inside these ranges and needn't reach their ends.
Inputs may be any that keep to these rules, and one draw needn't show every extreme that they name: `points`: coordinates lie in the unit cube. `landmarks`: coordinates lie in the unit cube.
All inputs are finite; a program needn't handle non-finite values.
Results may differ from the reference program's by a relative error of at most 0.00025.
Values sent between devices are 32-bit elements; how exact they have to be, the bound alone decides.
A program may use at most 128 MiB of HBM per device.

```python
import math
import jax
import jax.numpy as jnp
from jax import lax

RANK = 256
NODES = 7
BRANCHES = 64
TOTAL = 524288
N_BRANCH = 64


def draw_points(key, part):
    columns = jnp.arange(TOTAL)
    slab = (columns // (TOTAL // BRANCHES)).astype(jnp.float32)
    sample = jax.random.uniform(key, (3, TOTAL), jnp.float32)
    first = (slab + sample[0]) / BRANCHES
    return jnp.concatenate([first[None, :], sample[1:]], axis=0)


def draw_landmarks(key, part):
    regions = jnp.array([1.0, 2.0, 2.0, 4.0, 4.0, 4.0, 4.0], jnp.float32)
    places = jnp.array([0.0, 0.0, 1.0, 0.0, 1.0, 2.0, 3.0], jnp.float32)
    sample = jax.random.uniform(key, (NODES, 3, RANK), jnp.float32)
    first = (places[:, None] + sample[:, 0, :]) / regions[:, None]
    return jnp.concatenate([first[:, None, :], sample[:, 1:, :]], axis=1)


def block_levels(own_key, shape, cuts, least, high):
    level, own = 1.0, jax.random.fold_in(own_key, 6)
    for dim, blocks in cuts:
        steps = jnp.exp(jax.random.uniform(jax.random.fold_in(own, dim), (blocks,), jnp.float32, least / len(cuts), high / len(cuts)))
        level = level * jnp.repeat(steps, shape[dim] // blocks).reshape([-1 if axis == dim else 1 for axis in range(len(shape))])
    return level


def centred(key, dims, width, limit, kind=jnp.bfloat16):
    values = width * jax.random.normal(key, dims, jnp.float32)
    return jnp.clip(values, min=-limit, max=limit).astype(kind)


def setup_inputs(seed: int = 0) -> dict:
    splits = jax.random.split(jax.random.key(seed), 5)
    return {
        "points": draw_points(jax.random.fold_in(splits[4], 71), 0),
        "noise": jnp.clip(jnp.exp(math.log(2.0) - 2.3025851 * jax.random.uniform(splits[1], (TOTAL,), jnp.float32) ** block_levels(splits[1], (TOTAL,), ((0, 256),), -0.2, 0.2)), 0.2, 2.0),
        "landmarks": draw_landmarks(jax.random.fold_in(splits[4], 71), 0),
        "mixing": centred(splits[3], (NODES, RANK, RANK), 1.0, 6.0, jnp.float32),
    }


highest = lax.Precision.HIGHEST

def kernel_block(positions, landmark_set, length_scale):
    spread = jnp.zeros((positions.shape[1], landmark_set.shape[1]), jnp.float32)
    for component in range(3):
        offset = positions[component][:, None] - landmark_set[component][None, :]
        spread = spread + offset * offset
    return jnp.exp(-spread / (2.0 * length_scale * length_scale))

def node_products(left, right, node_count):
    left_nodes = left.reshape(node_count, -1, left.shape[1])
    right_nodes = right.reshape(node_count, -1, right.shape[1])
    return jnp.einsum('cnr,cns->crs', left_nodes.astype(jnp.float32), right_nodes.astype(jnp.float32), precision=highest, preferred_element_type=jnp.float32)

def apply_nodes(left, coefficients, node_count):
    left_nodes = left.reshape(node_count, -1, left.shape[1])
    result = jnp.einsum('cnr,crs->cns', left_nodes.astype(jnp.float32), coefficients.astype(jnp.float32), precision=highest, preferred_element_type=jnp.float32)
    return result.reshape(left.shape[0], coefficients.shape[2])

def solve_with(factor, right_side):
    return jax.scipy.linalg.cho_solve((factor, True), right_side)

def reference(points, noise, landmarks, mixing):
    width_rank = mixing.shape[1]
    total_rows = points.shape[1]
    length_scale = 0.6 * width_rank ** (-1.0 / 3.0)
    identity = jnp.eye(width_rank, dtype=jnp.float32)
    unit_list = []
    counts = []
    node_rows = []
    for level_index in range(3):
        node_count = 2 ** (2 - level_index)
        rows_each = total_rows // node_count
        pieces = []
        for node_index in range(node_count):
            node_id = node_count - 1 + node_index
            chosen = points[:, node_index * rows_each:(node_index + 1) * rows_each]
            kernel = kernel_block(chosen, landmarks[node_id], length_scale)
            pieces.append(jnp.dot(kernel.astype(jnp.float32), mixing[node_id].astype(jnp.float32), precision=highest, preferred_element_type=jnp.float32))
        unit_list.append(jnp.concatenate(pieces, axis=0))
        counts.append(node_count)
        node_rows.append(float(rows_each))
    bases = []
    factor_list = []
    for level_index in range(3):
        current = unit_list[level_index] / noise[:, None]
        for prior_index in range(level_index):
            cross = node_products(bases[prior_index], unit_list[level_index], counts[prior_index])
            coefficients = jax.vmap(solve_with)(factor_list[prior_index], cross) / node_rows[prior_index]
            current = current - apply_nodes(bases[prior_index], coefficients, counts[prior_index])
        bases.append(current)
        gram_matrix = node_products(current, unit_list[level_index], counts[level_index])
        factor_list.append(jnp.linalg.cholesky(identity[None] + gram_matrix / node_rows[level_index]))
    spread_factors = [jnp.repeat(factor, N_BRANCH // counts[index], axis=0) for index, factor in enumerate(factor_list)]
    return (jnp.stack(bases, axis=0), jnp.stack(spread_factors, axis=1))
```

```python
import functools

import jax
import jax.numpy as jnp
from jax import lax
from jax.experimental import pallas as pl
from jax.experimental.pallas import tpu as pltpu
from jax.sharding import PartitionSpec as P

f32 = jnp.float32
bf16 = jnp.bfloat16
highest = lax.Precision.HIGHEST
MESH = pl.DeviceIdType.MESH
RANK = 256
HALF = 128
CHIPS = 32
SLAB = 8
NODE_BRANCHES = 16
CHUNK = 256


def mm(left, right, contract=(1, 0)):
    return lax.dot_general(
        left, right, (((contract[0],), (contract[1],)), ((), ())),
        precision=highest, preferred_element_type=f32,
    )


def place():
    branch = lax.axis_index("branch")
    row = lax.axis_index("rows")
    chip = lax.rem(branch, NODE_BRANCHES) * 2 + row // 2
    return branch, row, chip, lax.rem(row, 2)


def chip_id(branch, chip, core):
    base = branch - lax.rem(branch, NODE_BRANCHES)
    return (base + chip // 2, lax.rem(chip, 2) * 2 + core)


def rows_kernel(scale, ids, points, noise, landmarks, m1, m2, m3, scaled, products):
    step = pl.program_id(0)
    columns = jnp.concatenate(
        [points[...], noise[...], jnp.zeros((4, CHUNK), f32)], axis=0
    ).T
    weight = 1.0 / columns[:, 3:4]
    units, weighted = [], []
    for level, mixing in enumerate((m1, m2, m3)):
        spread = None
        for c in range(3):
            mark = landmarks[pl.ds(ids[level], 1), c, :]
            offset = columns[:, c:c + 1] - mark
            spread = offset * offset if spread is None else spread + offset * offset
        kernel = jnp.exp(-spread * scale)
        unit = mm(kernel, mixing[0])
        units.append(unit)
        weighted.append(unit * weight)
        scaled[level] = weighted[level]

    @pl.when(step == 0)
    def _():
        products[...] = jnp.zeros_like(products)

    for index, (i, j) in enumerate(PAIRS):
        product = mm(weighted[i], units[j], (0, 0))
        products[0, index] += product[:, :HALF]
        products[1, index] += product[:, HALF:]


PAIRS = ((0, 0), (0, 1), (0, 2), (1, 1), (1, 2), (2, 2))


def local_rows(ids, points, noise, landmarks, mixing):
    rows = points.shape[1]
    length_scale = 0.6 * RANK ** (-1.0 / 3.0)
    scale = 1.0 / (2.0 * length_scale * length_scale)
    mix = [
        pl.BlockSpec((1, RANK, RANK), functools.partial(lambda n, i, ids: (ids[n], 0, 0), n))
        for n in range(3)
    ]
    return pl.pallas_call(
        functools.partial(rows_kernel, scale),
        grid_spec=pltpu.PrefetchScalarGridSpec(
            num_scalar_prefetch=1,
            grid=(rows // CHUNK,),
            in_specs=[
                pl.BlockSpec((3, CHUNK), lambda i, ids: (0, i)),
                pl.BlockSpec((1, CHUNK), lambda i, ids: (0, i)),
                pl.BlockSpec((7, 3, RANK), lambda i, ids: (0, 0, 0)),
            ] + mix,
            out_specs=[
                pl.BlockSpec((3, CHUNK, RANK), lambda i, ids: (0, i, 0)),
                pl.BlockSpec((2, 6, RANK, HALF), lambda i, ids: (0, 0, 0, 0)),
            ],
        ),
        out_shape=[
            jax.ShapeDtypeStruct((3, rows, RANK), f32),
            jax.ShapeDtypeStruct((2, 6, RANK, HALF), f32),
        ],
        name="local_rows",
    )(ids, points, noise[None], landmarks, mixing, mixing, mixing)


def greet(peers):
    barrier = pltpu.get_barrier_semaphore()
    for peer in peers:
        pl.semaphore_signal(barrier, inc=1, device_id=peer, device_id_type=MESH)
    return len(peers)


def greet_chips(branch, chip, core):
    barrier = pltpu.get_barrier_semaphore()

    def one(k, carry):
        pl.semaphore_signal(
            barrier, inc=1, device_id=chip_id(branch, chip ^ k, core), device_id_type=MESH
        )
        return carry

    lax.fori_loop(1, CHIPS, one, 0)


def send(src, dst, send_sem, recv_sem, peer):
    copy = pltpu.make_async_remote_copy(
        src_ref=src, dst_ref=dst, send_sem=send_sem, recv_sem=recv_sem,
        device_id=peer, device_id_type=MESH,
    )
    copy.start()
    return copy


def gather_slabs(full, mine, branch, chip, core, other, sems, first):
    rows = pl.ds(pl.multiple_of(chip * SLAB, SLAB), SLAB)
    full[core, :, rows, :] = mine[...]

    def one(k, carry):
        send(mine, full.at[core, :, rows, :], sems.at[first], sems.at[first + 1],
             chip_id(branch, chip ^ k, core))
        return carry

    lax.fori_loop(1, CHIPS, one, 0)
    rest = full.at[core, :, pl.ds(0, RANK - SLAB), :]
    pltpu.make_async_copy(rest, rest, sems.at[first + 1]).wait()
    pltpu.make_async_copy(rest, rest, sems.at[first]).wait()
    send(full.at[core], full.at[core], sems.at[first + 2], sems.at[first + 3], other).wait()


def reduce_kernel(products, full, slab, paired, total, landed, mine, sems):
    branch, row, chip, core = place()
    other = (branch, row + 1 - 2 * core)
    n = greet([other])
    greet_chips(branch, chip, core)
    pl.semaphore_wait(pltpu.get_barrier_semaphore(), n + CHIPS - 1)
    send(products.at[1 - core], paired, sems.at[0], sems.at[1], other).wait()
    total[...] = products[core] + paired[...]

    def one(k, carry):
        peer = chip ^ k
        rows = pl.ds(pl.multiple_of(peer * SLAB, SLAB), SLAB)
        send(total.at[:, rows, :], landed.at[k], sems.at[2], sems.at[3],
             chip_id(branch, peer, core))
        return carry

    lax.fori_loop(1, CHIPS, one, 0)
    rest = landed.at[pl.ds(1, CHIPS - 1)]
    pltpu.make_async_copy(rest, rest, sems.at[3]).wait()
    pltpu.make_async_copy(rest, rest, sems.at[2]).wait()
    value = total[:, pl.ds(pl.multiple_of(chip * SLAB, SLAB), SLAB), :]
    for k in range(1, CHIPS):
        value = value + landed[k]
    mine[...] = value[:3]
    slab[...] = value[3:]
    gather_slabs(full, mine, branch, chip, core, other, sems, 4)


def reduce_products(products):
    return pl.pallas_call(
        reduce_kernel,
        out_shape=[
            jax.ShapeDtypeStruct((2, 3, RANK, HALF), f32),
            jax.ShapeDtypeStruct((3, SLAB, HALF), f32),
        ],
        in_specs=[pl.BlockSpec(memory_space=pltpu.VMEM)],
        out_specs=[pl.BlockSpec(memory_space=pltpu.VMEM)] * 2,
        scratch_shapes=[
            pltpu.VMEM((6, RANK, HALF), f32),
            pltpu.VMEM((6, RANK, HALF), f32),
            pltpu.VMEM((CHIPS, 6, SLAB, HALF), f32),
            pltpu.VMEM((3, SLAB, HALF), f32),
            pltpu.SemaphoreType.DMA((8,)),
        ],
        compiler_params=pltpu.CompilerParams(collective_id=0, has_side_effects=True),
        name="reduce_products",
    )(products)


def join_kernel(bit, gathered, slabs, *refs):
    if gathered < slabs.shape[0]:
        full, slab, landed, mine, sems = refs
    else:
        full, landed, mine, sems = refs
    branch, row, chip, core = place()
    other = (branch, row + 1 - 2 * core)
    match = (branch ^ bit, row)
    n = greet([other, match])
    greet_chips(branch, chip, core)
    pl.semaphore_wait(pltpu.get_barrier_semaphore(), n + CHIPS - 1)
    send(slabs, landed, sems.at[0], sems.at[1], match).wait()
    value = slabs[...] + landed[...]
    mine[...] = value[:gathered]
    if gathered < slabs.shape[0]:
        slab[...] = value[gathered:]
    gather_slabs(full, mine, branch, chip, core, other, sems, 2)


def join_halves(slabs, bit, gathered, number):
    count = slabs.shape[0]
    out = [jax.ShapeDtypeStruct((2, gathered, RANK, HALF), f32)]
    if gathered < count:
        out.append(jax.ShapeDtypeStruct((count - gathered, SLAB, HALF), f32))
    return pl.pallas_call(
        functools.partial(join_kernel, bit, gathered),
        out_shape=out,
        in_specs=[pl.BlockSpec(memory_space=pltpu.VMEM)],
        out_specs=[pl.BlockSpec(memory_space=pltpu.VMEM)] * len(out),
        scratch_shapes=[
            pltpu.VMEM((count, SLAB, HALF), f32),
            pltpu.VMEM((gathered, SLAB, HALF), f32),
            pltpu.SemaphoreType.DMA((6,)),
        ],
        compiler_params=pltpu.CompilerParams(collective_id=number, has_side_effects=True),
        name="join_halves",
    )(slabs)


def split3(x):
    a = x.astype(bf16); r = x - a.astype(f32)
    b = r.astype(bf16); c = (r - b.astype(f32)).astype(bf16)
    return a, b, c

def factor(T, W):
    def super_panel(s, carry):
        r0 = pl.multiple_of(s * 32, 32)
        tile = pl.multiple_of((s // 4) * 128, 128)
        block = T[pl.ds(r0, 32), pl.ds(tile, 128)]
        W[:, 0:128] = pltpu.roll(block, lax.rem(128 - lax.rem(s, 4) * 32, 128), 1)
        W[:, 128:640] = T[pl.ds(r0, 32), :]
        for p in range(4):
            k0 = 8 * p
            cols = [jnp.broadcast_to(W[k0:32, k0 + m:k0 + m + 1], (32 - k0, 128)) for m in range(8)]
            e = {}
            for m in range(8):
                for i in range(m, 8):
                    e[i, m] = jnp.broadcast_to(cols[m][i:i + 1, :], (8, 128))
            r, l = {}, {}
            for j in range(8):
                r[j] = lax.rsqrt(e[j, j])
                for i in range(j + 1, 8):
                    l[i, j] = e[i, j] * r[j]
                for k in range(j + 1, 8):
                    for i in range(k, 8):
                        e[i, k] = e[i, k] - l[i, j] * l[k, j]
            rows = []
            for i in range(8):
                tiles = []
                for c in range(5):
                    w = jnp.broadcast_to(W[k0 + i:k0 + i + 1, c * 128:(c + 1) * 128], (8, 128))
                    for k in range(i):
                        w = w - l[i, k] * rows[k][c]
                    tiles.append(w * r[i])
                rows.append(tiles)
            below = []
            for t in range(1, 4 - p):
                lc = []
                for j in range(8):
                    v = cols[j][8 * t:8 * t + 8, :]
                    for k in range(j):
                        v = v - l[j, k] * lc[k]
                    lc.append(v * r[j])
                for c in range(5):
                    w = W[k0 + 8 * t:k0 + 8 * t + 8, c * 128:(c + 1) * 128]
                    for j in range(8):
                        w = w - lc[j] * rows[j][c]
                    W[k0 + 8 * t:k0 + 8 * t + 8, c * 128:(c + 1) * 128] = w
            for i in range(8):
                for c in range(5):
                    W[k0 + i:k0 + i + 1, c * 128:(c + 1) * 128] = rows[i][c][0:1, :]
        done = W[:, 128:640]
        T[pl.ds(r0, 32), :] = done
        a, b, c = split3(done)
        left = jnp.concatenate([a, a, b, b, a, c], axis=0)
        right = jnp.concatenate([a, b, a, b, c, a], axis=0)
        def update(half):
            lo = half * 128
            prod = lax.dot_general(left[:, lo:lo + 128], right, (((0,), (0,)), ((), ())),
                                   preferred_element_type=f32)
            row = lax.broadcasted_iota(jnp.int32, (128, 512), 0) + lo
            T[lo:lo + 128, :] = T[lo:lo + 128, :] - jnp.where(row >= r0 + 32, prod, 0.0)
        @pl.when(s < 3)
        def _():
            update(0)
        @pl.when(s < 7)
        def _():
            update(1)
        return carry
    lax.fori_loop(0, 8, super_panel, 0)

def factor_capacitance(gram, rows, lower, T, W):
    i0 = lax.broadcasted_iota(jnp.int32, (RANK, RANK), 0)
    i1 = lax.broadcasted_iota(jnp.int32, (RANK, RANK), 1)
    identity = jnp.where(i0 == i1, 1.0, 0.0)
    T[:, 0:RANK] = identity + gram / rows
    T[:, RANK:2 * RANK] = identity
    factor(T, W)
    lower[...] = jnp.where(i0 >= i1, T[:, 0:RANK].T, 0.0)
    return T[:, RANK:2 * RANK]


def whole(full, index):
    return jnp.concatenate([full[0, index], full[1, index]], axis=1)


def minus(slab, left, right, rows, spare, chip, core):
    product = mm(left, right, (0, 0)) / rows
    spare[0] = product[:, :HALF]
    spare[1] = product[:, HALF:]
    return slab - spare[core, pl.ds(pl.multiple_of(chip * SLAB, SLAB), SLAB), :]


def finest_kernel(rows, full, slab, lower, c12, c13, left, T, W, spare):
    branch, row, chip, core = place()
    inverse = factor_capacitance(whole(full, 0), rows, lower, T, W)
    y12 = mm(inverse, whole(full, 1))
    y13 = mm(inverse, whole(full, 2))
    left[0] = minus(slab[0], y12, y12, rows, spare, chip, core)
    left[1] = minus(slab[1], y12, y13, rows, spare, chip, core)
    left[2] = minus(slab[2], y13, y13, rows, spare, chip, core)
    c12[...] = mm(inverse, y12, (0, 0)) / rows
    c13[...] = mm(inverse, y13, (0, 0)) / rows


def middle_kernel(rows, full, slab, lower, c23, left, T, W, spare):
    branch, row, chip, core = place()
    inverse = factor_capacitance(whole(full, 0), rows, lower, T, W)
    y23 = mm(inverse, whole(full, 1))
    left[0] = minus(slab[0], y23, y23, rows, spare, chip, core)
    c23[...] = mm(inverse, y23, (0, 0)) / rows


def coarsest_kernel(rows, full, lower, T, W):
    factor_capacitance(whole(full, 0), rows, lower, T, W)


def small(kernel, rows, args, outs, spare):
    scratch = [pltpu.VMEM((RANK, 2 * RANK), f32), pltpu.VMEM((32, 640), f32)]
    if spare:
        scratch.append(pltpu.VMEM((2, RANK, HALF), f32))
    return pl.pallas_call(
        functools.partial(kernel, rows),
        out_shape=[jax.ShapeDtypeStruct(o, f32) for o in outs],
        in_specs=[pl.BlockSpec(memory_space=pltpu.VMEM)] * len(args),
        out_specs=[pl.BlockSpec(memory_space=pltpu.VMEM)] * len(outs),
        scratch_shapes=scratch,
        name=kernel.__name__,
    )(*args)


def bases_kernel(scaled, c12, c13, c23, bases):
    first = scaled[0]
    second = scaled[1] - mm(first, c12[...])
    third = scaled[2] - mm(first, c13[...]) - mm(second, c23[...])
    bases[0] = first
    bases[1] = second
    bases[2] = third


def solve_bases(scaled, c12, c13, c23):
    rows = scaled.shape[1]
    square = pl.BlockSpec((RANK, RANK), lambda i: (0, 0))
    block = pl.BlockSpec((3, CHUNK, RANK), lambda i: (0, i, 0))
    return pl.pallas_call(
        bases_kernel,
        grid=(rows // CHUNK,),
        in_specs=[block, square, square, square],
        out_specs=block,
        out_shape=jax.ShapeDtypeStruct(scaled.shape, f32),
        name="solve_bases",
    )(scaled, c12, c13, c23)


def on_device(points, noise, landmarks, mixing):
    branch = lax.axis_index("branch")
    node_rows = float(NODE_BRANCHES * lax.axis_size("rows") * points.shape[1])
    ids = jnp.stack([3 + branch // 16, 1 + branch // 32, 0 * branch]).astype(jnp.int32)
    scaled, products = local_rows(ids, points, noise, landmarks, mixing)
    full, slab = reduce_products(products)
    square = (RANK, RANK)
    l1, c12, c13, left = small(
        finest_kernel, node_rows, (full, slab), (square, square, square, (3, SLAB, HALF)), True
    )
    full, slab = join_halves(left, 16, 2, 1)
    l2, c23, left = small(
        middle_kernel, 2 * node_rows, (full, slab), (square, square, (1, SLAB, HALF)), True
    )
    (full,) = join_halves(left, 32, 1, 2)
    (l3,) = small(coarsest_kernel, 4 * node_rows, (full,), (square,), False)
    bases = solve_bases(scaled, c12, c13, c23)
    return bases, jnp.stack([l1, l2, l3], axis=0)[None]


def solution(mesh):
    in_specs = (P(None, ("branch", "rows")), P(("branch", "rows")), P(), P())
    out_specs = (P(None, ("branch", "rows"), None), P("branch", None, None, None))
    return jax.shard_map(
        on_device, mesh=mesh, in_specs=in_specs, out_specs=out_specs, check_vma=False
    )
```

```python
import functools

import jax
import jax.numpy as jnp
from jax import lax
from jax.experimental import pallas as pl
from jax.experimental.pallas import tpu as pltpu
from jax.sharding import PartitionSpec as P

f32 = jnp.float32
bf16 = jnp.bfloat16
highest = lax.Precision.HIGHEST
MESH = pl.DeviceIdType.MESH
RANK = 256
HALF = 128
CHIPS = 32
SLAB = 8
NODE_BRANCHES = 16
CHUNK = 512
BLOCKS = ((0, 0), (0, 1), (1, 1), (0, 2), (1, 2), (2, 2))
BATCHES = ((0, 1), (1, 3), (3, 6))


def mm(left, right, contract=(1, 0)):
    return lax.dot_general(
        left, right, (((contract[0],), (contract[1],)), ((), ())),
        precision=highest, preferred_element_type=f32,
    )


def place():
    branch = lax.axis_index("branch")
    row = lax.axis_index("rows")
    chip = lax.rem(branch, NODE_BRANCHES) * 2 + row // 2
    return branch, row, chip, lax.rem(row, 2)


def chip_id(branch, chip, core):
    base = branch - lax.rem(branch, NODE_BRANCHES)
    return (base + chip // 2, lax.rem(chip, 2) * 2 + core)


def split2(x):
    high = x.astype(bf16)
    return high, (x - high.astype(f32)).astype(bf16)


def split3(x):
    a = x.astype(bf16)
    r = x - a.astype(f32)
    b = r.astype(bf16)
    return a, b, (r - b.astype(f32)).astype(bf16)


def left3(parts, axis):
    return jnp.concatenate([parts[0], parts[0], parts[1]], axis=axis)


def right3(parts):
    return jnp.concatenate([parts[0], parts[1], parts[0]], axis=0)


def dot(left, right, contract=(1, 0)):
    return lax.dot_general(
        left, right, (((contract[0],), (contract[1],)), ((), ())), preferred_element_type=f32
    )


def super_panel(s, second, wide, T, W):
    r0 = pl.multiple_of(s * 32, 32)
    shift = lax.rem(s, 4) * 32
    own = HALF if second else 0
    others = [] if second else [HALF]
    if wide:
        others = others + ([2 * HALF, 3 * HALF] if second else [2 * HALF])
    count = 1 + len(others)
    W[:, 0:HALF] = pltpu.roll(T[pl.ds(r0, 32), own:own + HALF], lax.rem(HALF - shift, HALF), 1)
    for c, lane in enumerate(others):
        W[:, (c + 1) * HALF:(c + 2) * HALF] = T[pl.ds(r0, 32), lane:lane + HALF]
    for p in range(4):
        k0 = 8 * p
        cols = [
            jnp.broadcast_to(W[k0:32, k0 + m:k0 + m + 1], (32 - k0, HALF)) for m in range(8)
        ]
        e = {}
        for m in range(8):
            for i in range(m, 8):
                e[i, m] = jnp.broadcast_to(cols[m][i:i + 1, :], (8, HALF))
        r, l = {}, {}
        for j in range(8):
            r[j] = lax.rsqrt(e[j, j])
            for i in range(j + 1, 8):
                l[i, j] = e[i, j] * r[j]
            for k in range(j + 1, 8):
                for i in range(k, 8):
                    e[i, k] = e[i, k] - l[i, j] * l[k, j]
        rows = []
        for i in range(8):
            tiles = []
            for c in range(count):
                lanes = slice(c * HALF, (c + 1) * HALF)
                w = jnp.broadcast_to(W[k0 + i:k0 + i + 1, lanes], (8, HALF))
                for k in range(i):
                    w = w - l[i, k] * rows[k][c]
                tiles.append(w * r[i])
            rows.append(tiles)
        for t in range(1, 4 - p):
            lc = []
            for j in range(8):
                v = cols[j][8 * t:8 * t + 8, :]
                for k in range(j):
                    v = v - l[j, k] * lc[k]
                lc.append(v * r[j])
            for c in range(count):
                at = (slice(k0 + 8 * t, k0 + 8 * t + 8), slice(c * HALF, (c + 1) * HALF))
                w = W[at]
                for j in range(8):
                    w = w - lc[j] * rows[j][c]
                W[at] = w
        for i in range(8):
            for c in range(count):
                W[k0 + i:k0 + i + 1, c * HALF:(c + 1) * HALF] = rows[i][c][0:1, :]
    T[pl.ds(r0, 32), own:own + HALF] = pltpu.roll(W[:, 0:HALF], shift, 1)
    for c, lane in enumerate(others):
        T[pl.ds(r0, 32), lane:lane + HALF] = W[:, (c + 1) * HALF:(c + 2) * HALF]
    end = others[-1] + HALF if others else own + HALF
    a, b, c = split3(T[pl.ds(r0, 32), own:end])
    left = jnp.concatenate([a, a, b, b, a, c], axis=0)
    right = jnp.concatenate([a, b, a, b, c, a], axis=0)

    def update(first, lane):
        lo = lane - own
        product = dot(left[:, first - own:first - own + HALF], right[:, lo:], (0, 0))
        row = lax.broadcasted_iota(jnp.int32, product.shape, 0) + first
        T[first:first + HALF, lane:end] = (
            T[first:first + HALF, lane:end] - jnp.where(row >= r0 + 32, product, 0.0)
        )

    if second:
        @pl.when(s < 7)
        def _():
            update(HALF, HALF)
    else:
        @pl.when(s < 3)
        def _():
            update(0, 0)
        update(HALF, HALF)


def identity_matrix():
    i0 = lax.broadcasted_iota(jnp.int32, (RANK, RANK), 0)
    i1 = lax.broadcasted_iota(jnp.int32, (RANK, RANK), 1)
    return jnp.where(i0 == i1, 1.0, 0.0), i0 >= i1


def factor_capacitance(gram, rows, lower, T, W, hooks):
    identity, below = identity_matrix()
    T[:, 0:RANK] = identity + gram / rows
    T[:, RANK:2 * RANK] = identity

    def step(second, s, carry):
        for at, hook in hooks.items():
            if (at >= 4) == second:
                pl.when(s == at)(hook)
        super_panel(s, second, True, T, W)
        return carry

    lax.fori_loop(0, 4, functools.partial(step, False), 0)
    lax.fori_loop(4, 8, functools.partial(step, True), 0)
    lower[...] = jnp.where(below, T[:, 0:RANK].T, 0.0)
    return T[:, RANK:2 * RANK]


def send(src, dst, sems, at, peer):
    copy = pltpu.make_async_remote_copy(
        src_ref=src, dst_ref=dst, send_sem=sems.at[at], recv_sem=sems.at[at + 1],
        device_id=peer, device_id_type=MESH,
    )
    return copy


def drain(ref, sems, at):
    pltpu.make_async_copy(ref, ref, sems.at[at + 1]).wait()
    pltpu.make_async_copy(ref, ref, sems.at[at]).wait()


def chain_kernel(scale, node_rows, points, noise, landmarks, mixing,
                 bases, lower1, lower2, last,
                 cols, mix, V, VT, U, products, paired, total, landed, mine, full,
                 part, got, spare, T, W, sems, local):
    branch, row, chip, core = place()
    other = (branch, row + 1 - 2 * core)
    halves = ((branch ^ 16, row), (branch ^ 32, row))
    slab = pl.ds(pl.multiple_of(chip * SLAB, SLAB), SLAB)
    ids = (3 + branch // 16, 1 + branch // 32, 0)
    barrier = pltpu.get_barrier_semaphore()

    def loads(level):
        return pltpu.make_async_copy(mixing.at[ids[level]], mix.at[level], local.at[level])

    for level in range(3):
        loads(level).start()
    for peer in (other,) + halves:
        pl.semaphore_signal(barrier, inc=1, device_id=peer, device_id_type=MESH)

    def each_chip(action):
        def one(k, carry):
            action(k, chip ^ k)
            return carry
        lax.fori_loop(1, CHIPS, one, 0)

    each_chip(lambda k, peer: pl.semaphore_signal(
        barrier, inc=1, device_id=chip_id(branch, peer, core), device_id_type=MESH))

    def pair(batch):
        lo, hi = BATCHES[batch]
        return send(products.at[1 - core, lo:hi], paired.at[lo:hi], sems, 4 * batch, other)

    def scatter(batch):
        lo, hi = BATCHES[batch]
        pair(batch).wait()
        total[lo:hi] = products[core, lo:hi] + paired[lo:hi]

        def one(k, peer):
            rows = pl.ds(pl.multiple_of(peer * SLAB, SLAB), SLAB)
            send(total.at[lo:hi, rows, :], landed.at[k, lo:hi], sems, 4 * batch + 2,
                 chip_id(branch, peer, core)).start()
        each_chip(one)

    def collect(batch):
        lo, hi = BATCHES[batch]
        drain(landed.at[1:CHIPS, lo:hi], sems, 4 * batch + 2)
        value = total[lo:hi, slab, :]
        for k in range(1, CHIPS):
            value = value + landed[k, lo:hi]
        mine[lo:hi] = value

    def spread(g, ref):
        full[g, core, slab, :] = ref[...]
        each_chip(lambda k, peer: send(
            ref, full.at[g, core, slab, :], sems, 12 + 4 * g, chip_id(branch, peer, core)).start())

    def swap(g):
        return send(full.at[g, core], full.at[g, core], sems, 14 + 4 * g, other)

    def spread_done(g):
        drain(full.at[g, core, 0:RANK - SLAB, :], sems, 12 + 4 * g)
        swap(g).start()

    def match(at, lo, hi, peer):
        return send(part.at[lo:hi], got.at[lo:hi], sems, 36 + 2 * at, peer)

    def whole(g):
        return jnp.concatenate([full[g, 0], full[g, 1]], axis=1)

    def put(level):
        return pltpu.make_async_copy(V.at[level], bases.at[level], local.at[3 + level])

    chunks = V.shape[1] // CHUNK

    def loop(action):
        def one(i, carry):
            action(pl.ds(pl.multiple_of(i * CHUNK, CHUNK), CHUNK))
            return carry
        lax.fori_loop(0, chunks, one, 0)

    def unit(level):
        loads(level).wait()
        right = right3(split2(mix[level]))
        marks = [landmarks[pl.ds(ids[level], 1), c, :] for c in range(3)]

        def chunk(rows):
            spread_now = None
            for c in range(3):
                offset = cols[rows, c:c + 1] - marks[c]
                square = offset * offset
                spread_now = square if spread_now is None else spread_now + square
            kernel = jnp.exp(-spread_now * scale)
            value = dot(left3(split2(kernel), 1), right)
            weighted = value * (1.0 / cols[rows, 3:4])
            V[level, rows, :] = weighted
            for n, piece in enumerate(split2(value)):
                U[n, rows, :] = piece
            for n, piece in enumerate(split2(weighted)):
                VT[level, n, :, rows] = piece.T
        loop(chunk)

    def multiply(batch):
        lo, hi = BATCHES[batch]
        products[:, lo:hi] = jnp.zeros((2, hi - lo, RANK, HALF), f32)

        def chunk(rows):
            right = right3((U[0, rows, :], U[1, rows, :]))
            for b in range(lo, hi):
                i = BLOCKS[b][0]
                product = dot(left3((VT[i, 0, :, rows], VT[i, 1, :, rows]), 1), right)
                products[0, b] += product[:, :HALF]
                products[1, b] += product[:, HALF:]
        loop(chunk)

    cols[...] = jnp.concatenate(
        [points[...], noise[...], jnp.zeros((4, V.shape[1]), f32)], axis=0).T
    unit(0)
    multiply(0)
    pl.semaphore_wait(barrier, 3 + CHIPS - 1)
    pair(0).start()
    put(0).start()
    unit(1)
    scatter(0)
    multiply(1)
    pair(1).start()
    unit(2)
    collect(0)
    spread(0, mine.at[0])
    scatter(1)
    multiply(2)
    pair(2).start()
    spread_done(0)
    swap(0).wait()

    def late_scatter():
        scatter(2)

    def second_cross():
        collect(1)
        spread(1, mine.at[1])

    def third_cross():
        spread_done(1)
        collect(2)
        spread(2, mine.at[3])

    def minus(value, left, right, rows):
        product = mm(left, right, (0, 0)) / rows
        spare[0] = product[:, :HALF]
        spare[1] = product[:, HALF:]
        return value - spare[core, slab, :]

    inverse = factor_capacitance(
        whole(0), node_rows, lower1, T, W, {0: late_scatter, 2: second_cross, 6: third_cross})
    swap(1).wait()
    y12 = mm(inverse, whole(1))
    part[0] = minus(mine[2], y12, y12, node_rows)
    match(0, 0, 1, halves[0]).start()
    c12 = right3(split2(mm(inverse, y12, (0, 0)) / node_rows))

    match(0, 0, 1, halves[0]).wait()
    mine[0] = part[0] + got[0]
    spread(3, mine.at[0])
    spread_done(2)
    swap(2).wait()
    y13 = mm(inverse, whole(2))
    part[1] = minus(mine[4], y12, y13, node_rows)
    part[2] = minus(mine[5], y13, y13, node_rows)
    match(1, 1, 3, halves[0]).start()
    c13 = right3(split2(mm(inverse, y13, (0, 0)) / node_rows))
    spread_done(3)

    def second(rows):
        left = left3(split2(V[0, rows, :]), 1)
        V[1, rows, :] = V[1, rows, :] - dot(left, c12)
        V[2, rows, :] = V[2, rows, :] - dot(left, c13)
    loop(second)
    put(1).start()
    swap(3).wait()

    def cross_match():
        match(1, 1, 3, halves[0]).wait()
        mine[1:3] = part[1:3] + got[1:3]
        spread(4, mine.at[1])

    def cross_swap():
        spread_done(4)

    inverse = factor_capacitance(
        whole(3), 2.0 * node_rows, lower2, T, W, {1: cross_match, 6: cross_swap})
    swap(4).wait()
    y23 = mm(inverse, whole(4))
    part[3] = minus(mine[2], y23, y23, 2.0 * node_rows)
    match(2, 3, 4, halves[1]).start()
    c23 = right3(split2(mm(inverse, y23, (0, 0)) / (2.0 * node_rows)))
    match(2, 3, 4, halves[1]).wait()
    mine[3] = part[3] + got[3]
    spread(5, mine.at[3])

    def third(rows):
        V[2, rows, :] = V[2, rows, :] - dot(left3(split2(V[1, rows, :]), 1), c23)
    loop(third)
    put(2).start()
    spread_done(5)
    swap(5).wait()
    last[...] = full[5]
    for level in range(3):
        put(level).wait()


def chain(points, noise, landmarks, mixing, node_rows):
    rows = points.shape[1]
    length_scale = 0.6 * RANK ** (-1.0 / 3.0)
    scale = 1.0 / (2.0 * length_scale * length_scale)
    vmem = pl.BlockSpec(memory_space=pltpu.VMEM)
    hbm = pl.BlockSpec(memory_space=pl.ANY)
    square = jax.ShapeDtypeStruct((RANK, RANK), f32)
    return pl.pallas_call(
        functools.partial(chain_kernel, scale, node_rows),
        in_specs=[vmem, vmem, vmem, hbm],
        out_specs=[hbm, vmem, vmem, vmem],
        out_shape=[
            jax.ShapeDtypeStruct((3, rows, RANK), f32), square, square,
            jax.ShapeDtypeStruct((2, RANK, HALF), f32),
        ],
        scratch_shapes=[
            pltpu.VMEM((rows, 8), f32),
            pltpu.VMEM((3, RANK, RANK), f32),
            pltpu.VMEM((3, rows, RANK), f32),
            pltpu.VMEM((3, 2, RANK, rows), bf16),
            pltpu.VMEM((2, rows, RANK), bf16),
            pltpu.VMEM((2, 6, RANK, HALF), f32),
            pltpu.VMEM((6, RANK, HALF), f32),
            pltpu.VMEM((6, RANK, HALF), f32),
            pltpu.VMEM((CHIPS, 6, SLAB, HALF), f32),
            pltpu.VMEM((6, SLAB, HALF), f32),
            pltpu.VMEM((6, 2, RANK, HALF), f32),
            pltpu.VMEM((4, SLAB, HALF), f32),
            pltpu.VMEM((4, SLAB, HALF), f32),
            pltpu.VMEM((2, RANK, HALF), f32),
            pltpu.VMEM((RANK, 2 * RANK), f32),
            pltpu.VMEM((32, 4 * HALF), f32),
            pltpu.SemaphoreType.DMA((42,)),
            pltpu.SemaphoreType.DMA((6,)),
        ],
        compiler_params=pltpu.CompilerParams(
            collective_id=0, has_side_effects=True, vmem_limit_bytes=48 * 1024 * 1024),
        name="chain",
    )(points, noise[None], landmarks, mixing)


def finish_kernel(rows, solved, lower1, lower2, gram, bases, factors, T, W):
    s = pl.program_id(0)
    bases[...] = solved[...]

    @pl.when(s == 0)
    def _():
        T[...] = identity_matrix()[0] + jnp.concatenate([gram[0], gram[1]], axis=1) / rows
        factors[0, 0] = lower1[...]
        factors[0, 1] = lower2[...]

    @pl.when(s < 4)
    def _():
        super_panel(s, False, False, T, W)

    @pl.when(s >= 4)
    def _():
        super_panel(s, True, False, T, W)

    @pl.when(s == 7)
    def _():
        factors[0, 2] = jnp.where(identity_matrix()[1], T[...].T, 0.0)


def finish(solved, lower1, lower2, gram, rows):
    square = pl.BlockSpec((RANK, RANK), lambda i: (0, 0))
    block = pl.BlockSpec((3, solved.shape[1] // 8, RANK), lambda i: (0, i, 0))
    return pl.pallas_call(
        functools.partial(finish_kernel, rows),
        grid=(8,),
        in_specs=[block, square, square, pl.BlockSpec((2, RANK, HALF), lambda i: (0, 0, 0))],
        out_specs=[block, pl.BlockSpec((1, 3, RANK, RANK), lambda i: (0, 0, 0, 0))],
        out_shape=[
            jax.ShapeDtypeStruct(solved.shape, f32),
            jax.ShapeDtypeStruct((1, 3, RANK, RANK), f32),
        ],
        scratch_shapes=[pltpu.VMEM((RANK, RANK), f32), pltpu.VMEM((32, 2 * HALF), f32)],
        name="finish",
    )(solved, lower1, lower2, gram)


def on_device(points, noise, landmarks, mixing):
    node_rows = float(NODE_BRANCHES * lax.axis_size("rows") * points.shape[1])
    solved, lower1, lower2, gram = chain(points, noise, landmarks, mixing, node_rows)
    return tuple(finish(solved, lower1, lower2, gram, 4.0 * node_rows))


def solution(mesh):
    in_specs = (P(None, ("branch", "rows")), P(("branch", "rows")), P(), P())
    out_specs = (P(None, ("branch", "rows"), None), P("branch", None, None, None))
    return jax.shard_map(
        on_device, mesh=mesh, in_specs=in_specs, out_specs=out_specs, check_vma=False
    )
```

```python
import functools

import jax
import jax.numpy as jnp
from jax import lax
from jax.experimental import pallas as pl
from jax.experimental.pallas import tpu as pltpu
from jax.sharding import PartitionSpec as P

f32 = jnp.float32
bf16 = jnp.bfloat16
highest = lax.Precision.HIGHEST
MESH = pl.DeviceIdType.MESH
RANK = 256
HALF = 128
CHIPS = 32
SLAB = 8
NODE_BRANCHES = 16
CHUNK = 512
BLOCKS = ((0, 0), (0, 1), (1, 1), (0, 2), (1, 2), (2, 2))
FACTOR_SCRATCH = (pltpu.VMEM((32, 32, HALF), f32), pltpu.VMEM((8, 32, HALF), f32))
BATCHES = ((0, 1), (1, 3), (3, 6))


def mm(left, right, contract=(1, 0)):
    return lax.dot_general(
        left, right, (((contract[0],), (contract[1],)), ((), ())),
        precision=highest, preferred_element_type=f32,
    )


def place():
    branch = lax.axis_index("branch")
    row = lax.axis_index("rows")
    chip = lax.rem(branch, NODE_BRANCHES) * 2 + row // 2
    return branch, row, chip, lax.rem(row, 2)


def chip_id(branch, chip, core):
    base = branch - lax.rem(branch, NODE_BRANCHES)
    return (base + chip // 2, lax.rem(chip, 2) * 2 + core)


def split2(x):
    high = x.astype(bf16)
    return high, (x - high.astype(f32)).astype(bf16)


def split3(x):
    a = x.astype(bf16)
    r = x - a.astype(f32)
    b = r.astype(bf16)
    return a, b, (r - b.astype(f32)).astype(bf16)


def left3(parts, axis):
    return jnp.concatenate([parts[0], parts[0], parts[1]], axis=axis)


def right3(parts):
    return jnp.concatenate([parts[0], parts[1], parts[0]], axis=0)


def dot(left, right, contract=(1, 0)):
    return lax.dot_general(
        left, right, (((contract[0],), (contract[1],)), ((), ())), preferred_element_type=f32
    )


def super_panel(s, second, wide, T, W, C, M):
    r0 = pl.multiple_of(s * 32, 32)
    shift = lax.rem(s, 4) * 32
    own = HALF if second else 0
    others = [] if second else [HALF]
    if wide:
        others = others + ([2 * HALF, 3 * HALF] if second else [2 * HALF])
    count = 1 + len(others)
    lanes_of = [own] + others
    for c, lane in enumerate(lanes_of):
        W[:, c * HALF:(c + 1) * HALF] = T[pl.ds(r0, 32), lane:lane + HALF]
    square = W[:, 0:HALF]
    for q in range(4):
        for m in range(8):
            C[8 * q + m, 8 * q:32] = jnp.take_along_axis(
                square[8 * q:32], jnp.full((32 - 8 * q, HALF), shift + 8 * q + m, jnp.int32), axis=1)
    for p in range(4):
        k0 = 8 * p
        e = {}
        for m in range(8):
            for i in range(m, 8):
                e[i, m] = jnp.broadcast_to(C[k0 + m, k0 + i:k0 + i + 1, :], (8, HALF))
        r, l = {}, {}
        for j in range(8):
            r[j] = lax.rsqrt(e[j, j])
            for i in range(j + 1, 8):
                l[i, j] = e[i, j] * r[j]
            for k in range(j + 1, 8):
                for i in range(k, 8):
                    e[i, k] = e[i, k] - l[i, j] * l[k, j]
        lower = {}
        for t in range(p + 1, 4):
            for j in range(8):
                v = C[k0 + j, 8 * t:8 * t + 8, :]
                for k in range(j):
                    v = v - l[j, k] * lower[t, k]
                lower[t, j] = v * r[j]
                M[j, 8 * t:8 * t + 8, :] = lower[t, j]
        for q in range(p + 1, 4):
            for m in range(8):
                across = [
                    jnp.broadcast_to(M[j, 8 * q + m:8 * q + m + 1, :], (8, HALF)) for j in range(8)
                ]
                for t in range(q, 4):
                    at = (8 * q + m, slice(8 * t, 8 * t + 8))
                    v = C[at]
                    for j in range(8):
                        v = v - lower[t, j] * across[j]
                    C[at] = v
        rows = []
        for i in range(8):
            tiles = []
            for c in range(count):
                lanes = slice(c * HALF, (c + 1) * HALF)
                w = jnp.broadcast_to(W[k0 + i:k0 + i + 1, lanes], (8, HALF))
                for k in range(i):
                    w = w - l[i, k] * rows[k][c]
                tiles.append(w * r[i])
            rows.append(tiles)
        for t in range(p + 1, 4):
            for c in range(count):
                at = (slice(8 * t, 8 * t + 8), slice(c * HALF, (c + 1) * HALF))
                w = W[at]
                for j in range(8):
                    w = w - lower[t, j] * rows[j][c]
                W[at] = w
        for i in range(8):
            for c in range(count):
                W[k0 + i:k0 + i + 1, c * HALF:(c + 1) * HALF] = rows[i][c][0:1, :]
    for c, lane in enumerate(lanes_of):
        T[pl.ds(r0, 32), lane:lane + HALF] = W[:, c * HALF:(c + 1) * HALF]
    end = others[-1] + HALF if others else own + HALF
    a, b, c = split3(T[pl.ds(r0, 32), own:end])
    left = jnp.concatenate([a, a, b, b, a, c], axis=0)
    right = jnp.concatenate([a, b, a, b, c, a], axis=0)

    def update(first, lane):
        lo = lane - own
        product = dot(left[:, first - own:first - own + HALF], right[:, lo:], (0, 0))
        row = lax.broadcasted_iota(jnp.int32, product.shape, 0) + first
        T[first:first + HALF, lane:end] = (
            T[first:first + HALF, lane:end] - jnp.where(row >= r0 + 32, product, 0.0)
        )

    if second:
        @pl.when(s < 7)
        def _():
            update(HALF, HALF)
    else:
        @pl.when(s < 3)
        def _():
            update(0, 0)
        update(HALF, HALF)


def identity_matrix():
    i0 = lax.broadcasted_iota(jnp.int32, (RANK, RANK), 0)
    i1 = lax.broadcasted_iota(jnp.int32, (RANK, RANK), 1)
    return jnp.where(i0 == i1, 1.0, 0.0), i0 >= i1


def factor_capacitance(gram, rows, lower, T, W, C, M, hooks):
    identity, below = identity_matrix()
    T[:, 0:RANK] = identity + gram / rows
    T[:, RANK:2 * RANK] = identity

    def step(second, s, carry):
        for at, hook in hooks.items():
            if (at >= 4) == second:
                pl.when(s == at)(hook)
        super_panel(s, second, True, T, W, C, M)
        return carry

    lax.fori_loop(0, 4, functools.partial(step, False), 0)
    lax.fori_loop(4, 8, functools.partial(step, True), 0)
    lower[...] = jnp.where(below, T[:, 0:RANK].T, 0.0)
    return T[:, RANK:2 * RANK]


def send(src, dst, sems, at, peer):
    copy = pltpu.make_async_remote_copy(
        src_ref=src, dst_ref=dst, send_sem=sems.at[at], recv_sem=sems.at[at + 1],
        device_id=peer, device_id_type=MESH,
    )
    return copy


def drain(ref, sems, at):
    pltpu.make_async_copy(ref, ref, sems.at[at + 1]).wait()
    pltpu.make_async_copy(ref, ref, sems.at[at]).wait()


def chain_kernel(scale, node_rows, points, noise, landmarks, mixing,
                 bases, lower1_out, lower2_out, last_out,
                 points_in, noise_in, marks_in, lower1, lower2, cols, mix, V, VT, U, products, paired, total, landed, mine, full,
                 part, got, spare, T, W, C, M, sems, local):
    branch, row, chip, core = place()
    other = (branch, row + 1 - 2 * core)
    halves = ((branch ^ 16, row), (branch ^ 32, row))
    slab = pl.ds(pl.multiple_of(chip * SLAB, SLAB), SLAB)
    ids = (3 + branch // 16, 1 + branch // 32, 0)
    barrier = pltpu.get_barrier_semaphore()

    def loads(level):
        return pltpu.make_async_copy(mixing.at[ids[level]], mix.at[level], local.at[level])

    inputs = [
        pltpu.make_async_copy(src, dst, local.at[6 + n]) for n, (src, dst) in enumerate(
            ((points, points_in), (noise, noise_in), (landmarks, marks_in)))
    ]
    for copy in inputs:
        copy.start()
    for level in range(3):
        loads(level).start()
    for peer in (other,) + halves:
        pl.semaphore_signal(barrier, inc=1, device_id=peer, device_id_type=MESH)

    def each_chip(action):
        def one(k, carry):
            action(k, chip ^ k)
            return carry
        lax.fori_loop(1, CHIPS, one, 0)

    each_chip(lambda k, peer: pl.semaphore_signal(
        barrier, inc=1, device_id=chip_id(branch, peer, core), device_id_type=MESH))

    def pair(batch):
        lo, hi = BATCHES[batch]
        return send(products.at[1 - core, lo:hi], paired.at[lo:hi], sems, 4 * batch, other)

    def scatter(batch):
        lo, hi = BATCHES[batch]
        pair(batch).wait()
        total[lo:hi] = products[core, lo:hi] + paired[lo:hi]

        def one(k, peer):
            rows = pl.ds(pl.multiple_of(peer * SLAB, SLAB), SLAB)
            send(total.at[lo:hi, rows, :], landed.at[k, lo:hi], sems, 4 * batch + 2,
                 chip_id(branch, peer, core)).start()
        each_chip(one)

    def collect(batch):
        lo, hi = BATCHES[batch]
        drain(landed.at[1:CHIPS, lo:hi], sems, 4 * batch + 2)
        value = total[lo:hi, slab, :]
        for k in range(1, CHIPS):
            value = value + landed[k, lo:hi]
        mine[lo:hi] = value

    def spread(g, ref):
        full[g, core, slab, :] = ref[...]
        each_chip(lambda k, peer: send(
            ref, full.at[g, core, slab, :], sems, 12 + 4 * g, chip_id(branch, peer, core)).start())

    def swap(g):
        return send(full.at[g, core], full.at[g, core], sems, 14 + 4 * g, other)

    def spread_done(g):
        drain(full.at[g, core, 0:RANK - SLAB, :], sems, 12 + 4 * g)
        swap(g).start()

    def match(at, lo, hi, peer):
        return send(part.at[lo:hi], got.at[lo:hi], sems, 36 + 2 * at, peer)

    def whole(g):
        return jnp.concatenate([full[g, 0], full[g, 1]], axis=1)

    def put(level):
        return pltpu.make_async_copy(V.at[level], bases.at[level], local.at[3 + level])

    chunks = V.shape[1] // CHUNK

    def loop(action):
        def one(i, carry):
            action(pl.ds(pl.multiple_of(i * CHUNK, CHUNK), CHUNK))
            return carry
        lax.fori_loop(0, chunks, one, 0)

    def unit(level):
        loads(level).wait()
        right = right3(split2(mix[level]))
        marks = [marks_in[c, pl.ds(ids[level], 1), :] for c in range(3)]

        def chunk(rows):
            spread_now = None
            for c in range(3):
                offset = cols[rows, c:c + 1] - marks[c]
                square = offset * offset
                spread_now = square if spread_now is None else spread_now + square
            kernel = jnp.exp(-spread_now * scale)
            value = dot(left3(split2(kernel), 1), right)
            weighted = value * (1.0 / cols[rows, 3:4])
            V[level, rows, :] = weighted
            for n, piece in enumerate(split2(value)):
                U[n, rows, :] = piece
            for n, piece in enumerate(split2(weighted)):
                VT[level, n, :, rows] = piece.T
        loop(chunk)

    def multiply(batch):
        lo, hi = BATCHES[batch]
        products[:, lo:hi] = jnp.zeros((2, hi - lo, RANK, HALF), f32)

        def chunk(rows):
            right = right3((U[0, rows, :], U[1, rows, :]))
            for b in range(lo, hi):
                i = BLOCKS[b][0]
                product = dot(left3((VT[i, 0, :, rows], VT[i, 1, :, rows]), 1), right)
                products[0, b] += product[:, :HALF]
                products[1, b] += product[:, HALF:]
        loop(chunk)

    for copy in inputs:
        copy.wait()
    cols[...] = jnp.concatenate(
        [points_in[...], noise_in[...], jnp.zeros((4, V.shape[1]), f32)], axis=0).T
    unit(0)
    multiply(0)
    pl.semaphore_wait(barrier, 3 + CHIPS - 1)
    pair(0).start()
    put(0).start()
    unit(1)
    scatter(0)
    multiply(1)
    pair(1).start()
    unit(2)
    collect(0)
    spread(0, mine.at[0])
    scatter(1)
    multiply(2)
    pair(2).start()
    spread_done(0)
    swap(0).wait()

    def late_scatter():
        scatter(2)

    def second_cross():
        collect(1)
        spread(1, mine.at[1])

    def third_cross():
        spread_done(1)
        collect(2)
        spread(2, mine.at[3])

    def minus(value, left, right, rows):
        product = mm(left, right, (0, 0)) / rows
        spare[0] = product[:, :HALF]
        spare[1] = product[:, HALF:]
        return value - spare[core, slab, :]

    inverse = factor_capacitance(
        whole(0), node_rows, lower1, T, W, C, M, {0: late_scatter, 2: second_cross, 6: third_cross})
    put_lower1 = pltpu.make_async_copy(lower1, lower1_out, local.at[9])
    put_lower1.start()
    swap(1).wait()
    y12 = mm(inverse, whole(1))
    part[0] = minus(mine[2], y12, y12, node_rows)
    match(0, 0, 1, halves[0]).start()
    c12 = right3(split2(mm(inverse, y12, (0, 0)) / node_rows))

    match(0, 0, 1, halves[0]).wait()
    mine[0] = part[0] + got[0]
    spread(3, mine.at[0])
    spread_done(2)
    swap(2).wait()
    y13 = mm(inverse, whole(2))
    part[1] = minus(mine[4], y12, y13, node_rows)
    part[2] = minus(mine[5], y13, y13, node_rows)
    match(1, 1, 3, halves[0]).start()
    c13 = right3(split2(mm(inverse, y13, (0, 0)) / node_rows))
    spread_done(3)

    def second(rows):
        left = left3(split2(V[0, rows, :]), 1)
        V[1, rows, :] = V[1, rows, :] - dot(left, c12)
        V[2, rows, :] = V[2, rows, :] - dot(left, c13)
    loop(second)
    put(1).start()
    swap(3).wait()

    def cross_match():
        match(1, 1, 3, halves[0]).wait()
        mine[1:3] = part[1:3] + got[1:3]
        spread(4, mine.at[1])

    def cross_swap():
        spread_done(4)

    inverse = factor_capacitance(
        whole(3), 2.0 * node_rows, lower2, T, W, C, M, {1: cross_match, 6: cross_swap})
    put_lower2 = pltpu.make_async_copy(lower2, lower2_out, local.at[10])
    put_lower2.start()
    swap(4).wait()
    y23 = mm(inverse, whole(4))
    part[3] = minus(mine[2], y23, y23, 2.0 * node_rows)
    match(2, 3, 4, halves[1]).start()
    c23 = right3(split2(mm(inverse, y23, (0, 0)) / (2.0 * node_rows)))
    match(2, 3, 4, halves[1]).wait()
    mine[3] = part[3] + got[3]
    spread(5, mine.at[3])

    def third(rows):
        V[2, rows, :] = V[2, rows, :] - dot(left3(split2(V[1, rows, :]), 1), c23)
    loop(third)
    put(2).start()
    spread_done(5)
    swap(5).wait()
    put_last = pltpu.make_async_copy(full.at[5], last_out, local.at[11])
    put_last.start()
    for level in range(3):
        put(level).wait()
    put_lower1.wait()
    put_lower2.wait()
    put_last.wait()


def chain(points, noise, landmarks, mixing, node_rows):
    rows = points.shape[1]
    length_scale = 0.6 * RANK ** (-1.0 / 3.0)
    scale = 1.0 / (2.0 * length_scale * length_scale)
    hbm = pl.BlockSpec(memory_space=pl.ANY)
    square = jax.ShapeDtypeStruct((RANK, RANK), f32)
    return pl.pallas_call(
        functools.partial(chain_kernel, scale, node_rows),
        in_specs=[hbm] * 4,
        out_specs=[hbm] * 4,
        out_shape=[
            jax.ShapeDtypeStruct((3, rows, RANK), f32), square, square,
            jax.ShapeDtypeStruct((2, RANK, HALF), f32),
        ],
        scratch_shapes=[
            pltpu.VMEM((3, rows), f32),
            pltpu.VMEM((1, rows), f32),
            pltpu.VMEM((3, 7, RANK), f32),
            pltpu.VMEM((RANK, RANK), f32),
            pltpu.VMEM((RANK, RANK), f32),
            pltpu.VMEM((rows, 8), f32),
            pltpu.VMEM((3, RANK, RANK), f32),
            pltpu.VMEM((3, rows, RANK), f32),
            pltpu.VMEM((3, 2, RANK, rows), bf16),
            pltpu.VMEM((2, rows, RANK), bf16),
            pltpu.VMEM((2, 6, RANK, HALF), f32),
            pltpu.VMEM((6, RANK, HALF), f32),
            pltpu.VMEM((6, RANK, HALF), f32),
            pltpu.VMEM((CHIPS, 6, SLAB, HALF), f32),
            pltpu.VMEM((6, SLAB, HALF), f32),
            pltpu.VMEM((6, 2, RANK, HALF), f32),
            pltpu.VMEM((4, SLAB, HALF), f32),
            pltpu.VMEM((4, SLAB, HALF), f32),
            pltpu.VMEM((2, RANK, HALF), f32),
            pltpu.VMEM((RANK, 2 * RANK), f32),
            pltpu.VMEM((32, 4 * HALF), f32),
            pltpu.VMEM((32, 32, HALF), f32), pltpu.VMEM((8, 32, HALF), f32),
            pltpu.SemaphoreType.DMA((42,)),
            pltpu.SemaphoreType.DMA((12,)),
        ],
        compiler_params=pltpu.CompilerParams(
            collective_id=0, has_side_effects=True),
        name="chain",
    )(points, noise[None], jnp.transpose(landmarks, (1, 0, 2)), mixing)


def finish_kernel(rows, solved, lower1, lower2, gram, bases, factors, T, W, C, M):
    s = pl.program_id(0)
    bases[...] = solved[...]

    @pl.when(s == 0)
    def _():
        T[...] = identity_matrix()[0] + jnp.concatenate([gram[0], gram[1]], axis=1) / rows
        factors[0, 0] = lower1[...]
        factors[0, 1] = lower2[...]

    @pl.when(s < 4)
    def _():
        super_panel(s, False, False, T, W, C, M)

    @pl.when(s >= 4)
    def _():
        super_panel(s, True, False, T, W, C, M)

    @pl.when(s == 7)
    def _():
        factors[0, 2] = jnp.where(identity_matrix()[1], T[...].T, 0.0)


def finish(solved, lower1, lower2, gram, rows):
    square = pl.BlockSpec((RANK, RANK), lambda i: (0, 0))
    block = pl.BlockSpec((3, solved.shape[1] // 8, RANK), lambda i: (0, i, 0))
    return pl.pallas_call(
        functools.partial(finish_kernel, rows),
        grid=(8,),
        in_specs=[block, square, square, pl.BlockSpec((2, RANK, HALF), lambda i: (0, 0, 0))],
        out_specs=[block, pl.BlockSpec((1, 3, RANK, RANK), lambda i: (0, 0, 0, 0))],
        out_shape=[
            jax.ShapeDtypeStruct(solved.shape, f32),
            jax.ShapeDtypeStruct((1, 3, RANK, RANK), f32),
        ],
        scratch_shapes=[
            pltpu.VMEM((RANK, RANK), f32), pltpu.VMEM((32, 2 * HALF), f32),
            pltpu.VMEM((32, 32, HALF), f32), pltpu.VMEM((8, 32, HALF), f32),
        ],
        name="finish",
    )(solved, lower1, lower2, gram)


def on_device(points, noise, landmarks, mixing):
    node_rows = float(NODE_BRANCHES * lax.axis_size("rows") * points.shape[1])
    solved, lower1, lower2, gram = chain(points, noise, landmarks, mixing, node_rows)
    return tuple(finish(solved, lower1, lower2, gram, 4.0 * node_rows))


def solution(mesh):
    in_specs = (P(None, ("branch", "rows")), P(("branch", "rows")), P(), P())
    out_specs = (P(None, ("branch", "rows"), None), P("branch", None, None, None))
    return jax.shard_map(
        on_device, mesh=mesh, in_specs=in_specs, out_specs=out_specs, check_vma=False
    )
```
